32 devices in a mesh: wide: 16 (over z, x, core), narrow: 2 (over y).
Axes of the slice: x: 2, y: 2, z: 4, core: 2. Of those that a mesh axis runs over, the one named last changes fastest.
Arguments:
- tokens: bfloat16 [32, 128, 1024], P(('wide', 'narrow')), may hold values from -6 to 6
- lengths: int32 [32, 4], P(('wide', 'narrow')), may hold values from 1 to 64, 128 in all within a row
- w_query: bfloat16 [1024, 1024], P(('wide', 'narrow')), may hold values from -0.1875 to 0.1875
- w_key: bfloat16 [1024, 1024], P(('wide', 'narrow')), may hold values from -0.1875 to 0.1875
- w_value: bfloat16 [1024, 1024], P(('wide', 'narrow')), may hold values from -0.1875 to 0.1875
- w_out: bfloat16 [1024, 1024], P(('wide', 'narrow')), may hold values from -0.1875 to 0.1875
- w_up: bfloat16 [1024, 4096], P(('wide', 'narrow')), may hold values from -0.1875 to 0.1875
- w_down: bfloat16 [4096, 1024], P(('wide', 'narrow')), may hold values from -0.09375 to 0.09375
- gain_one: bfloat16 [1024], P(('wide', 'narrow')), may hold values from 0.5 to 1.5
- shift_one: bfloat16 [1024], P(('wide', 'narrow')), may hold values from -4 to 4
- gain_two: bfloat16 [1024], P(('wide', 'narrow')), may hold values from 0.5 to 1.5
- shift_two: bfloat16 [1024], P(('wide', 'narrow')), may hold values from -4 to 4
- gain_three: bfloat16 [1024], P(('wide', 'narrow')), may hold values from 0.5 to 1.5
- shift_three: bfloat16 [1024], P(('wide', 'narrow')), may hold values from -4 to 4
- gain_four: bfloat16 [1024], P(('wide', 'narrow')), may hold values from 0.5 to 1.5
- shift_four: bfloat16 [1024], P(('wide', 'narrow')), may hold values from -4 to 4
- cotangent: bfloat16 [32, 128, 1024], P(('wide', 'narrow')), may hold values from -6 to 6
Outputs:
- output: bfloat16 [32, 128, 1024], P(('wide', 'narrow'))
- input_grad: bfloat16 [32, 128, 1024], P(('wide', 'narrow'))
- grad_query: float32 [1024, 1024], P(('wide', 'narrow'))
- grad_key: float32 [1024, 1024], P(('wide', 'narrow'))
- grad_value: float32 [1024, 1024], P(('wide', 'narrow'))
- grad_out: float32 [1024, 1024], P(('wide', 'narrow'))
- grad_up: float32 [1024, 4096], P(('wide', 'narrow'))
- grad_down: float32 [4096, 1024], P(('wide', 'narrow'))
- grad_gain_one: float32 [1024], P(('wide', 'narrow'))
- grad_shift_one: float32 [1024], P(('wide', 'narrow'))
- grad_gain_two: float32 [1024], P(('wide', 'narrow'))
- grad_shift_two: float32 [1024], P(('wide', 'narrow'))
- grad_gain_three: float32 [1024], P(('wide', 'narrow'))
- grad_shift_three: float32 [1024], P(('wide', 'narrow'))
- grad_gain_four: float32 [1024], P(('wide', 'narrow'))
- grad_shift_four: float32 [1024], P(('wide', 'narrow'))
The draws below stay inside these ranges and needn't reach their ends.
Inputs may be any that keep to these rules, and one draw needn't show every extreme that they name: Each row's 4 lengths sum to 128; the longest in every row is 64.
All inputs are finite; a program needn't handle non-finite values.
Results may differ from the reference program's by a relative error of at most 0.014.
Values may be sent and summed in bfloat16 or wider, within the bound.
No kernel may reach another device: no remote copies, remote signals or barrier semaphores. Data moves between devices by JAX's collectives and lax.ppermute only.
A program may use at most 192 MiB of HBM per device.

```python
import math
from functools import partial
import jax
import jax.numpy as jnp
import numpy as np
from jax import lax

D = 1024
HEADS = 16
FF = 4096
ROW = 128
DOCS = 4
BATCH = 32


def block_scale(rng, extent, shards, low, top_value):
    factor_of = 1.0
    for axis_at, shards_of in shards:
        draws = jax.random.uniform(jax.random.fold_in(jax.random.fold_in(rng, 6), axis_at), (shards_of,), jnp.float32, low / len(shards), top_value / len(shards))
        factor_of = factor_of * jnp.repeat(jnp.exp(draws), extent[axis_at] // shards_of).reshape((-1,) + (1,) * (len(extent) - 1 - axis_at))
    return factor_of


def profile(number_of, total, limit, skew):
    portions = [(1 << 20) // math.isqrt(rank ** skew) + 1 for rank in range(2, number_of + 1)]
    spare, counts = total - limit - (number_of - 1), [1] * (number_of - 1)
    while spare > 0:
        free = [i for i in range(number_of - 1) if counts[i] < limit]
        mass, remaining = sum([portions[i] for i in free]), spare
        for i in free:
            more = min(limit - counts[i], max(1, remaining * portions[i] // mass), spare)
            counts[i] = counts[i] + more
            spare = spare - more
    return np.array([limit] + counts)


def ragged(key, count, total, most, slope):
    if count == 2:
        one = jax.random.randint(key, (), max(1, total - most), min(most, total - 1) + 1)
        return jnp.stack([one, total - one])
    tallies = jnp.asarray(profile(count, total, most, slope), jnp.int32)
    couples = (count - 1) // 2
    source_of, taker = tallies[1:1 + 2 * couples:2], tallies[2:2 + 2 * couples:2]
    room = jnp.minimum(source_of - 1, most - taker)
    moved = jax.random.randint(jax.random.fold_in(key, 1), (couples,), 0, 1 << 20) % (room + 1)
    tallies = tallies.at[1:1 + 2 * couples:2].set(source_of - moved).at[2:2 + 2 * couples:2].set(taker + moved)
    return tallies[jax.random.permutation(jax.random.fold_in(key, 2), count)]


def centred(key, shape, spread, most, split=(), kind=jnp.bfloat16):
    entries = spread * jax.random.normal(key, shape, jnp.float32)
    if split:
        entries = entries * block_scale(key, shape, split, -0.22, 0.18)
    return jnp.clip(entries, -most, most).astype(kind)


def setup_inputs(seed: int = 0) -> dict:
    arg_keys = jax.random.split(jax.random.key(seed), 18)
    tokens = centred(arg_keys[0], (BATCH, ROW, D), 1.0, 6.0, ((0, 32),))
    lengths = jax.vmap(lambda own: ragged(own, DOCS, ROW, ROW // 2, 2))(jax.random.split(arg_keys[1], BATCH)).reshape((BATCH, DOCS)).astype(jnp.int32)
    w_query = centred(arg_keys[2], (D, D), D ** -0.5, 0.1875, ((0, 32),))
    w_key = centred(arg_keys[3], (D, D), D ** -0.5, 0.1875, ((0, 32),))
    w_value = centred(arg_keys[4], (D, D), D ** -0.5, 0.1875, ((0, 32),))
    w_out = centred(arg_keys[5], (D, D), D ** -0.5, 0.1875, ((0, 32),))
    w_up = centred(arg_keys[6], (D, FF), D ** -0.5, 0.1875, ((0, 32),))
    w_down = centred(arg_keys[7], (FF, D), FF ** -0.5, 0.09375, ((0, 32),))
    gain_one = jnp.clip(1.0 + 0.1 * jax.random.normal(arg_keys[8], (D,), jnp.float32), 0.5, 1.5).astype(jnp.bfloat16)
    shift_one = centred(arg_keys[9], (D,), 0.3, 4.0, ((0, 32),))
    gain_two = jnp.clip(1.0 + 0.1 * jax.random.normal(arg_keys[10], (D,), jnp.float32), 0.5, 1.5).astype(jnp.bfloat16)
    shift_two = centred(arg_keys[11], (D,), 0.3, 4.0, ((0, 32),))
    gain_three = jnp.clip(1.0 + 0.1 * jax.random.normal(arg_keys[12], (D,), jnp.float32), 0.5, 1.5).astype(jnp.bfloat16)
    shift_three = centred(arg_keys[13], (D,), 0.3, 4.0, ((0, 32),))
    gain_four = jnp.clip(1.0 + 0.1 * jax.random.normal(arg_keys[14], (D,), jnp.float32), 0.5, 1.5).astype(jnp.bfloat16)
    shift_four = centred(arg_keys[15], (D,), 0.3, 4.0, ((0, 32),))
    cotangent = centred(arg_keys[16], (BATCH, ROW, D), 1.0, 6.0, ((0, 32),))
    return dict(tokens=tokens, lengths=lengths, w_query=w_query, w_key=w_key, w_value=w_value, w_out=w_out, w_up=w_up, w_down=w_down, gain_one=gain_one, shift_one=shift_one, gain_two=gain_two, shift_two=shift_two, gain_three=gain_three, shift_three=shift_three, gain_four=gain_four, shift_four=shift_four, cotangent=cotangent)


@jax.custom_vjp
def low(v):
    return lax.optimization_barrier(v.astype(jnp.bfloat16)).astype(jnp.float32)

@jax.custom_vjp
def low_back(v):
    return v

def low_keep(v):
    return (low(v), None)

def low_pass(kept, grad):
    return (grad,)

def back_keep(v):
    return (v, None)

def back_low(kept, grad):
    return (low(grad),)
low.defvjp(low_keep, low_pass)
low_back.defvjp(back_keep, back_low)
epsilon = 1e-05
highest = lax.Precision.HIGHEST

def layer_norm(value, gain, shift):
    center = value - lax.optimization_barrier(jnp.mean(value, -1, keepdims=True))
    inverse = lax.rsqrt(lax.optimization_barrier(jnp.mean(center * center, -1, keepdims=True)) + epsilon)
    return center * inverse * gain + shift

def doc_places(lengths, count):
    lengths = lengths.astype(jnp.int32)
    ends = jnp.cumsum(lengths).astype(jnp.int32)
    starts = (ends - lengths).astype(jnp.int32)
    places = jnp.arange(count, dtype=jnp.int32)
    doc_ids = lax.optimization_barrier(jnp.sum((places[:, None] >= ends[None, :]).astype(jnp.int32), 1)).astype(jnp.int32)
    owner = doc_ids[:, None] == jnp.arange(lengths.shape[0], dtype=jnp.int32)[None, :]
    first = lax.optimization_barrier(jnp.sum(jnp.where(owner, starts[None, :], 0), 1)).astype(jnp.int32)
    return (doc_ids, (places - first).astype(jnp.int32))

def rotary_tables(places, half):
    freqs = jnp.exp(jnp.arange(half, dtype=jnp.float32) * (-math.log(10000.0) / half))
    angles = places.astype(jnp.float32)[..., None] * freqs
    return (jnp.cos(angles), jnp.sin(angles))

def rotate(value, cos_table, sin_table):
    half = value.shape[-1] // 2
    front = value[..., :half]
    back = value[..., half:]
    cos_wide = cos_table[..., None, :]
    sin_wide = sin_table[..., None, :]
    return jnp.concatenate([front * cos_wide - back * sin_wide, back * cos_wide + front * sin_wide], -1)

def gelu_exact(value):
    return 0.5 * value * (1.0 + jax.scipy.special.erf(value * (1.0 / math.sqrt(2.0))))

def block_forward(tokens, w_query, w_key, w_value, w_out, w_up, w_down, gain_one, shift_one, gain_two, shift_two, gain_three, shift_three, gain_four, shift_four, cos_table, sin_table, visible):
    groups, rows, width = tokens.shape
    head_dim = width // HEADS
    normed_in = low(layer_norm(tokens, gain_one, shift_one))

    def project(weight):
        return low_back(jnp.einsum('gtd,de->gte', normed_in, weight, precision=highest)).reshape(groups, rows, HEADS, head_dim)
    queries = low(rotate(project(w_query), cos_table, sin_table))
    keys = low(rotate(project(w_key), cos_table, sin_table))
    values = low(project(w_value))
    raw = jnp.einsum('gqhe,gkhe->ghqk', queries, keys, precision=highest) * head_dim ** (-0.5)
    scores = jnp.where(visible[:, None], low_back(raw), -1e+30)
    top = lax.optimization_barrier(jnp.max(scores, -1, keepdims=True))
    expd = jnp.exp(scores - top)
    probs = expd / lax.optimization_barrier(jnp.sum(expd, -1, keepdims=True))
    mixed = low(low_back(jnp.einsum('ghqk,gkhe->gqhe', low(probs), values, precision=highest))).reshape(groups, rows, width)
    branch = low_back(jnp.einsum('gtd,de->gte', mixed, w_out, precision=highest))
    middle = tokens + layer_norm(branch, gain_two, shift_two)
    normed_mid = low(layer_norm(middle, gain_three, shift_three))
    hidden_pre = low_back(jnp.einsum('gtd,df->gtf', normed_mid, w_up, precision=highest))
    hidden = low(gelu_exact(hidden_pre))
    mlp_out = low_back(jnp.einsum('gtf,fd->gtd', hidden, w_down, precision=highest))
    return middle + layer_norm(mlp_out, gain_four, shift_four)

def reference(tokens, lengths, w_query, w_key, w_value, w_out, w_up, w_down, gain_one, shift_one, gain_two, shift_two, gain_three, shift_three, gain_four, shift_four, cotangent):
    weights = tuple((item.astype(jnp.float32) for item in (w_query, w_key, w_value, w_out, w_up, w_down, gain_one, shift_one, gain_two, shift_two, gain_three, shift_three, gain_four, shift_four)))
    batch, rows, width = tokens.shape
    group = max(1, min(batch, 4096 // rows))
    count = batch // group
    order = jnp.arange(rows, dtype=jnp.int32)

    def one_group(totals, item):
        block_in, block_len, block_cot = item
        doc_ids, places = jax.vmap(partial(doc_places, count=rows))(block_len)
        cos_table, sin_table = rotary_tables(places, width // HEADS // 2)
        visible = (doc_ids[:, :, None] == doc_ids[:, None, :]) & (order[None, None, :] <= order[None, :, None])

        def forward(value, *params):
            return block_forward(value, *params, cos_table, sin_table, visible)
        result, pull = jax.vjp(forward, block_in.astype(jnp.float32), *weights)
        grads = pull(block_cot.astype(jnp.float32))
        totals = tuple((total + extra for total, extra in zip(totals, grads[1:])))
        return (totals, (result.astype(jnp.bfloat16), grads[0].astype(jnp.bfloat16)))
    zeros = tuple((jnp.zeros(item.shape, jnp.float32) for item in weights))
    items = (tokens.reshape(count, group, rows, width), lengths.reshape(count, group, lengths.shape[-1]), cotangent.reshape(count, group, rows, width))
    totals, (outs, grads) = lax.scan(one_group, zeros, items)
    return (outs.reshape(batch, rows, width), grads.reshape(batch, rows, width), totals[0], totals[1], totals[2], totals[3], totals[4], totals[5], totals[6], totals[7], totals[8], totals[9], totals[10], totals[11], totals[12], totals[13])
```

```python
from functools import partial
import math

import jax
import jax.numpy as jnp
from jax import lax
from jax.sharding import PartitionSpec as P

HEADS = 16
AXES = ("wide", "narrow")


ROWS3, ROWS2, ROWS1 = P(AXES, None, None), P(AXES, None), P(AXES)
epsilon = 1e-05
group_heads = 4


def norm_forward(value, gain, shift):
    center = value - jnp.mean(value, -1, keepdims=True)
    inverse = lax.rsqrt(jnp.mean(center * center, -1, keepdims=True) + epsilon)
    normed = center * inverse
    return (normed * gain + shift, normed, inverse)


def norm_backward(upstream, normed, inverse, gain):
    scaled = upstream * gain
    inner = (
        scaled
        - jnp.mean(scaled, -1, keepdims=True)
        - normed * jnp.mean(scaled * normed, -1, keepdims=True)
    )
    return (inverse * inner, jnp.sum(upstream * normed, 0), jnp.sum(upstream, 0))


def doc_places(lengths, count):
    ends = jnp.cumsum(lengths)
    starts = ends - lengths
    places = jnp.arange(count, dtype=jnp.int32)
    doc_ids = jnp.sum((places[:, None] >= ends[None, :]).astype(jnp.int32), 1)
    owner = doc_ids[:, None] == jnp.arange(lengths.shape[0], dtype=jnp.int32)[None, :]
    first = jnp.sum(jnp.where(owner, starts[None, :], 0), 1)
    return (doc_ids, places - first)


def rotary_tables(places, half):
    freqs = jnp.exp(jnp.arange(half, dtype=jnp.float32) * (-math.log(10000.0) / half))
    angles = places.astype(jnp.float32)[..., None] * freqs
    return (jnp.cos(angles), jnp.sin(angles))


def rotate(value, cos_table, sin_table):
    half = value.shape[-1] // 2
    front = value[..., :half]
    back = value[..., half:]
    cos_wide = cos_table[:, None, :]
    sin_wide = sin_table[:, None, :]
    return jnp.concatenate(
        [front * cos_wide - back * sin_wide, back * cos_wide + front * sin_wide], -1
    )


def unrotate(upstream, cos_table, sin_table):
    half = upstream.shape[-1] // 2
    front = upstream[..., :half]
    back = upstream[..., half:]
    cos_wide = cos_table[:, None, :]
    sin_wide = sin_table[:, None, :]
    return jnp.concatenate(
        [front * cos_wide + back * sin_wide, back * cos_wide - front * sin_wide], -1
    )


def gelu_exact(value):
    return 0.5 * value * (1.0 + jax.scipy.special.erf(value * (1.0 / math.sqrt(2.0))))


def gelu_slope(value):
    return 0.5 * (1.0 + jax.scipy.special.erf(value * (1.0 / math.sqrt(2.0)))) + value * jnp.exp(
        -0.5 * value * value
    ) * (1.0 / math.sqrt(2.0 * math.pi))


def to_groups(value):
    rows, heads, depth = value.shape
    return value.reshape(rows, heads // group_heads, group_heads, depth).transpose(1, 2, 0, 3)


def from_groups(value):
    count, inner, rows, depth = value.shape
    return value.transpose(2, 0, 1, 3).reshape(rows, count * inner * depth)


def block_scores(query_block, key_block, visible, scale):
    scores = (
        jnp.einsum("hqe,hke->hqk", query_block, key_block, preferred_element_type=jnp.float32)
        * scale
    )
    return jnp.where(visible[None], scores, -1e30)


def attend(blocks, visible, scale):
    query_block, key_block, value_block = blocks
    scores = block_scores(query_block, key_block, visible, scale)
    top = jnp.max(scores, -1, keepdims=True)
    expd = jnp.exp(scores - top)
    total = jnp.sum(expd, -1, keepdims=True)
    probs = (expd / total).astype(jnp.bfloat16)
    mixed = jnp.einsum("hqk,hke->hqe", probs, value_block, preferred_element_type=jnp.float32)
    return (mixed, (top + jnp.log(total))[..., 0])


def attend_back(blocks, visible, scale):
    query_block, key_block, value_block, upstream, log_total = blocks
    scores = block_scores(query_block, key_block, visible, scale)
    probs = jnp.where(visible[None], jnp.exp(scores - log_total[..., None]), 0.0)
    grad_probs = jnp.einsum(
        "hqe,hke->hqk", upstream, value_block, preferred_element_type=jnp.float32
    )
    grad_values = jnp.einsum(
        "hqk,hqe->hke", probs.astype(jnp.bfloat16), upstream, preferred_element_type=jnp.float32
    )
    inner = jnp.sum(probs * grad_probs, -1, keepdims=True)
    grad_scores = (probs * (grad_probs - inner)).astype(jnp.bfloat16)
    grad_queries = (
        jnp.einsum("hqk,hke->hqe", grad_scores, key_block, preferred_element_type=jnp.float32)
        * scale
    )
    grad_keys = (
        jnp.einsum("hqk,hqe->hke", grad_scores, query_block, preferred_element_type=jnp.float32)
        * scale
    )
    return (grad_queries, grad_keys, grad_values)


def local_general(
    tokens,
    lengths,
    w_query,
    w_key,
    w_value,
    w_out,
    w_up,
    w_down,
    gain_one,
    shift_one,
    gain_two,
    shift_two,
    gain_three,
    shift_three,
    gain_four,
    shift_four,
    cotangent,
):
    inputs = tokens[0].astype(jnp.float32)
    rows, width = inputs.shape
    head_dim = width // HEADS
    scale = head_dim ** (-0.5)
    doc_ids, places = doc_places(lengths[0], rows)
    cos_table, sin_table = rotary_tables(places, head_dim // 2)
    order = jnp.arange(rows, dtype=jnp.int32)
    visible = (doc_ids[:, None] == doc_ids[None, :]) & (order[None, :] <= order[:, None])
    attn_parts = (
        lax.all_gather(w_query, AXES, axis=0, tiled=True),
        lax.all_gather(w_key, AXES, axis=0, tiled=True),
        lax.all_gather(w_value, AXES, axis=0, tiled=True),
        lax.all_gather(w_out, AXES, axis=0, tiled=True),
        lax.all_gather(gain_one, AXES, axis=0, tiled=True),
        lax.all_gather(shift_one, AXES, axis=0, tiled=True),
        lax.all_gather(gain_two, AXES, axis=0, tiled=True),
        lax.all_gather(shift_two, AXES, axis=0, tiled=True),
    )
    normed_one, unit_one, inv_one = norm_forward(
        inputs, attn_parts[4].astype(jnp.float32), attn_parts[5].astype(jnp.float32)
    )
    normed_low = normed_one.astype(jnp.bfloat16)

    def project(weight):
        return jnp.dot(normed_low, weight, preferred_element_type=jnp.float32).reshape(
            rows, HEADS, head_dim
        )

    queries = rotate(project(attn_parts[0]), cos_table, sin_table).astype(jnp.bfloat16)
    keys = rotate(project(attn_parts[1]), cos_table, sin_table).astype(jnp.bfloat16)
    values = project(attn_parts[2]).astype(jnp.bfloat16)
    query_groups = to_groups(queries)
    key_groups = to_groups(keys)
    value_groups = to_groups(values)
    mixed_groups, log_totals = lax.map(
        partial(attend, visible=visible, scale=scale), (query_groups, key_groups, value_groups)
    )
    mixed = from_groups(mixed_groups).astype(jnp.bfloat16)
    branch = jnp.dot(mixed, attn_parts[3], preferred_element_type=jnp.float32)
    normed_two, unit_two, inv_two = norm_forward(
        branch, attn_parts[6].astype(jnp.float32), attn_parts[7].astype(jnp.float32)
    )
    middle = inputs + normed_two
    mlp_parts = (
        lax.all_gather(w_up, AXES, axis=0, tiled=True),
        lax.all_gather(w_down, AXES, axis=0, tiled=True),
        lax.all_gather(gain_three, AXES, axis=0, tiled=True),
        lax.all_gather(shift_three, AXES, axis=0, tiled=True),
        lax.all_gather(gain_four, AXES, axis=0, tiled=True),
        lax.all_gather(shift_four, AXES, axis=0, tiled=True),
    )
    normed_three, unit_three, inv_three = norm_forward(
        middle, mlp_parts[2].astype(jnp.float32), mlp_parts[3].astype(jnp.float32)
    )
    normed_mid = normed_three.astype(jnp.bfloat16)
    hidden_pre = jnp.dot(normed_mid, mlp_parts[0], preferred_element_type=jnp.float32)
    hidden = gelu_exact(hidden_pre).astype(jnp.bfloat16)
    mlp_out = jnp.dot(hidden, mlp_parts[1], preferred_element_type=jnp.float32)
    normed_four, unit_four, inv_four = norm_forward(
        mlp_out, mlp_parts[4].astype(jnp.float32), mlp_parts[5].astype(jnp.float32)
    )
    result = middle + normed_four
    mlp_parts = (
        lax.all_gather(w_up, AXES, axis=0, tiled=True),
        lax.all_gather(w_down, AXES, axis=0, tiled=True),
        lax.all_gather(gain_three, AXES, axis=0, tiled=True),
        lax.all_gather(shift_three, AXES, axis=0, tiled=True),
        lax.all_gather(gain_four, AXES, axis=0, tiled=True),
        lax.all_gather(shift_four, AXES, axis=0, tiled=True),
    )
    upstream = cotangent[0].astype(jnp.float32)
    grad_mlp, grad_gain_four, grad_shift_four = norm_backward(
        upstream, unit_four, inv_four, mlp_parts[4].astype(jnp.float32)
    )
    grad_mlp_low = grad_mlp.astype(jnp.bfloat16)
    grad_w_down = jnp.einsum("tf,td->fd", hidden, grad_mlp_low, preferred_element_type=jnp.float32)
    grad_hidden = jnp.einsum(
        "td,fd->tf", grad_mlp_low, mlp_parts[1], preferred_element_type=jnp.float32
    )
    grad_pre = (grad_hidden * gelu_slope(hidden_pre)).astype(jnp.bfloat16)
    grad_w_up = jnp.einsum("td,tf->df", normed_mid, grad_pre, preferred_element_type=jnp.float32)
    grad_norm_three = jnp.einsum(
        "tf,df->td", grad_pre, mlp_parts[0], preferred_element_type=jnp.float32
    )
    grad_mid_part, grad_gain_three, grad_shift_three = norm_backward(
        grad_norm_three, unit_three, inv_three, mlp_parts[2].astype(jnp.float32)
    )
    grad_middle = upstream + grad_mid_part
    mlp_sums = (
        lax.psum_scatter(grad_w_up, AXES, scatter_dimension=0, tiled=True),
        lax.psum_scatter(grad_w_down, AXES, scatter_dimension=0, tiled=True),
        lax.psum_scatter(grad_gain_three, AXES, scatter_dimension=0, tiled=True),
        lax.psum_scatter(grad_shift_three, AXES, scatter_dimension=0, tiled=True),
        lax.psum_scatter(grad_gain_four, AXES, scatter_dimension=0, tiled=True),
        lax.psum_scatter(grad_shift_four, AXES, scatter_dimension=0, tiled=True),
    )
    attn_parts = (
        lax.all_gather(w_query, AXES, axis=0, tiled=True),
        lax.all_gather(w_key, AXES, axis=0, tiled=True),
        lax.all_gather(w_value, AXES, axis=0, tiled=True),
        lax.all_gather(w_out, AXES, axis=0, tiled=True),
        lax.all_gather(gain_one, AXES, axis=0, tiled=True),
        lax.all_gather(shift_one, AXES, axis=0, tiled=True),
        lax.all_gather(gain_two, AXES, axis=0, tiled=True),
        lax.all_gather(shift_two, AXES, axis=0, tiled=True),
    )
    grad_branch, grad_gain_two, grad_shift_two = norm_backward(
        grad_middle, unit_two, inv_two, attn_parts[6].astype(jnp.float32)
    )
    grad_branch_low = grad_branch.astype(jnp.bfloat16)
    grad_w_out = jnp.einsum("te,td->ed", mixed, grad_branch_low, preferred_element_type=jnp.float32)
    grad_mixed = jnp.einsum(
        "td,ed->te", grad_branch_low, attn_parts[3], preferred_element_type=jnp.float32
    ).astype(jnp.bfloat16)
    grad_mixed_groups = to_groups(grad_mixed.reshape(rows, HEADS, head_dim))
    grad_q_groups, grad_k_groups, grad_v_groups = lax.map(
        partial(attend_back, visible=visible, scale=scale),
        (query_groups, key_groups, value_groups, grad_mixed_groups, log_totals),
    )
    grad_queries = (
        unrotate(from_groups(grad_q_groups).reshape(rows, HEADS, head_dim), cos_table, sin_table)
        .reshape(rows, width)
        .astype(jnp.bfloat16)
    )
    grad_keys = (
        unrotate(from_groups(grad_k_groups).reshape(rows, HEADS, head_dim), cos_table, sin_table)
        .reshape(rows, width)
        .astype(jnp.bfloat16)
    )
    grad_values = from_groups(grad_v_groups).astype(jnp.bfloat16)
    grad_w_query = jnp.einsum(
        "td,te->de", normed_low, grad_queries, preferred_element_type=jnp.float32
    )
    grad_w_key = jnp.einsum("td,te->de", normed_low, grad_keys, preferred_element_type=jnp.float32)
    grad_w_value = jnp.einsum(
        "td,te->de", normed_low, grad_values, preferred_element_type=jnp.float32
    )
    grad_normed = jnp.einsum(
        "te,de->td", grad_queries, attn_parts[0], preferred_element_type=jnp.float32
    )
    grad_normed = grad_normed + jnp.einsum(
        "te,de->td", grad_keys, attn_parts[1], preferred_element_type=jnp.float32
    )
    grad_normed = grad_normed + jnp.einsum(
        "te,de->td", grad_values, attn_parts[2], preferred_element_type=jnp.float32
    )
    grad_in_part, grad_gain_one, grad_shift_one = norm_backward(
        grad_normed, unit_one, inv_one, attn_parts[4].astype(jnp.float32)
    )
    grad_input = grad_middle + grad_in_part
    attn_sums = (
        lax.psum_scatter(grad_w_query, AXES, scatter_dimension=0, tiled=True),
        lax.psum_scatter(grad_w_key, AXES, scatter_dimension=0, tiled=True),
        lax.psum_scatter(grad_w_value, AXES, scatter_dimension=0, tiled=True),
        lax.psum_scatter(grad_w_out, AXES, scatter_dimension=0, tiled=True),
        lax.psum_scatter(grad_gain_one, AXES, scatter_dimension=0, tiled=True),
        lax.psum_scatter(grad_shift_one, AXES, scatter_dimension=0, tiled=True),
        lax.psum_scatter(grad_gain_two, AXES, scatter_dimension=0, tiled=True),
        lax.psum_scatter(grad_shift_two, AXES, scatter_dimension=0, tiled=True),
    )
    return (
        result.astype(jnp.bfloat16)[None],
        grad_input.astype(jnp.bfloat16)[None],
        attn_sums[0],
        attn_sums[1],
        attn_sums[2],
        attn_sums[3],
        mlp_sums[0],
        mlp_sums[1],
        attn_sums[4],
        attn_sums[5],
        attn_sums[6],
        attn_sums[7],
        mlp_sums[2],
        mlp_sums[3],
        mlp_sums[4],
        mlp_sums[5],
    )


CORES = 2
SIDE = 2


def pack_fits(mesh, head_count):
    wide, narrow = mesh.shape["wide"], mesh.shape["narrow"]
    return narrow == SIDE and wide % (CORES * SIDE) == 0 and wide == head_count


class Grid:
    def __init__(self, wide, narrow):
        self.depth = wide // (CORES * SIDE)
        place = lax.axis_index("wide")
        self.z = place // (CORES * SIDE)
        self.x = (place // CORES) % SIDE
        self.c = place % CORES
        self.y = lax.axis_index("narrow")
        self.narrow = narrow

    def pairs(self, move):
        found = []
        for z in range(self.depth):
            for x in range(SIDE):
                for c in range(CORES):
                    for y in range(self.narrow):
                        to_z, to_x, to_c, to_y = move(z, x, c, y)
                        source = ((z * SIDE + x) * CORES + c) * self.narrow + y
                        target = ((to_z * SIDE + to_x) * CORES + to_c) * self.narrow + to_y
                        found.append((source, target))
        return found

    def over_core(self, value):
        return lax.ppermute(value, AXES, self.pairs(lambda z, x, c, y: (z, x, 1 - c, y)))

    def over_x(self, value):
        return lax.ppermute(value, AXES, self.pairs(lambda z, x, c, y: (z, 1 - x, c, y)))

    def over_y(self, value):
        return lax.ppermute(value, AXES, self.pairs(lambda z, x, c, y: (z, x, c, 1 - y)))

    def along_z(self, value, step):
        return lax.ppermute(
            value, AXES, self.pairs(lambda z, x, c, y: ((z + step) % self.depth, x, c, y))
        )


def put(buffer, block, starts):
    return lax.dynamic_update_slice(buffer, block, starts)


def gather_chips(grid, piece):
    depth = grid.depth
    column = jnp.zeros((depth,) + piece.shape, piece.dtype)
    column = put(column, piece[None], (grid.z, 0, 0))
    for step in range(1, depth):
        other = grid.along_z(piece, step)
        column = put(column, other[None], ((grid.z - step) % depth, 0, 0))
    side_x = grid.over_x(column)
    side_y = grid.over_y(column)
    half = depth // 2
    corner = jnp.concatenate([grid.over_x(side_y[:half]), grid.over_y(side_x[half:])], 0)
    return column, side_x, side_y, corner


def lay(grid, columns, pick, shape):
    own, side_x, side_y, corner = columns
    x, y = grid.x, grid.y
    buffer = jnp.zeros(shape, own.dtype)
    split = len(shape) == 6
    for column, at_x, at_y in (
        (own, x, y),
        (side_x, 1 - x, y),
        (side_y, x, 1 - y),
        (corner, 1 - x, 1 - y),
    ):
        block = pick(column)
        if split:
            buffer = put(buffer, block[:, None, :, None], (0, at_x, 0, at_y, 0, 0))
        else:
            buffer = put(buffer, block[:, None, None], (0, at_x, at_y, 0, 0))
    return buffer


def take(grid, value, at_x, at_y):
    if value.ndim == 6:
        depth, _, cores, _, rows, cols = value.shape
        part = lax.dynamic_slice(
            value, (0, at_x, 0, at_y, 0, 0), (depth, 1, cores, 1, rows, cols)
        )
        return part.reshape(depth, cores, rows, cols)
    depth, _, _, rows, cols = value.shape
    part = lax.dynamic_slice(value, (0, at_x, at_y, 0, 0), (depth, 1, 1, rows, cols))
    return part.reshape(depth, rows, cols)


def scatter_chips(grid, pack):
    depth = grid.depth
    half = depth // 2
    x, y = grid.x, grid.y
    corner = pack(1 - x, 1 - y)
    from_x = grid.over_x(corner[:half])
    from_y = grid.over_y(corner[half:])
    to_y = pack(x, 1 - y)
    to_x = pack(1 - x, y)
    to_y = jnp.concatenate([widen(to_y[:half]) + widen(from_x), widen(to_y[half:])], 0)
    to_x = jnp.concatenate([widen(to_x[:half]), widen(to_x[half:]) + widen(from_y)], 0)
    got_y = grid.over_y(to_y.astype(jnp.bfloat16))
    got_x = grid.over_x(to_x.astype(jnp.bfloat16))
    column = widen(pack(x, y)) + widen(got_y) + widen(got_x)
    low = column.astype(jnp.bfloat16)
    total = lax.dynamic_index_in_dim(column, grid.z, 0, False)
    for step in range(1, depth):
        send = lax.dynamic_index_in_dim(low, (grid.z + step) % depth, 0, False)
        total = total + widen(grid.along_z(send, step))
    return total


def widen(value):
    return value.astype(jnp.float32)


def by_core(grid, mine, other):
    first = jnp.where(grid.c == 0, mine, other)
    second = jnp.where(grid.c == 0, other, mine)
    return first, second


def share(grid, partial_sum):
    rows = partial_sum.shape[0] // CORES
    other = grid.over_core(partial_sum)
    return partial_sum + jnp.concatenate([other[rows:], other[:rows]], 0)


def split_heads(value, count):
    rows = value.shape[0] // CORES
    return value.reshape(CORES, rows, count, value.shape[1] // count)


def rotate_heads(value, cos_table, sin_table):
    half = value.shape[-1] // 2
    front, back = value[..., :half], value[..., half:]
    cos_wide, sin_wide = cos_table[:, :, None, :], sin_table[:, :, None, :]
    return jnp.concatenate(
        [front * cos_wide - back * sin_wide, back * cos_wide + front * sin_wide], -1
    )


def local_packed(
    wide,
    narrow,
    tokens,
    lengths,
    w_query,
    w_key,
    w_value,
    w_out,
    w_up,
    w_down,
    gain_one,
    shift_one,
    gain_two,
    shift_two,
    gain_three,
    shift_three,
    gain_four,
    shift_four,
    cotangent,
):
    grid = Grid(wide, narrow)
    depth = grid.depth
    bf16, f32 = jnp.bfloat16, jnp.float32
    _, rows, width = tokens.shape
    block = w_query.shape[0]
    hidden_width = w_up.shape[1]
    down_block = w_down.shape[0]
    head_dim = width // HEADS
    heads = HEADS // CORES
    part = width // CORES
    hidden_part = hidden_width // CORES
    wide_blocks = hidden_part // width
    scale = head_dim ** (-0.5)
    is_first = grid.c == 0

    def parities(value, unit):
        cut = value.reshape(value.shape[0], -1, CORES, unit)
        even, odd = cut[:, :, 0].reshape(value.shape[0], -1), cut[:, :, 1].reshape(value.shape[0], -1)
        return jnp.where(is_first, even, odd), jnp.where(is_first, odd, even)

    trio = jnp.concatenate([w_query, w_key, w_value], 0)
    trio_keep, trio_give = parities(trio, head_dim)
    up_keep, up_give = parities(w_up, hidden_width // wide)
    vectors = jnp.stack(
        [gain_one, shift_one, gain_two, shift_two, gain_three, shift_three, gain_four, shift_four]
    )
    trio_first, trio_second = by_core(grid, trio_keep, grid.over_core(trio_give))
    up_first, up_second = by_core(grid, up_keep, grid.over_core(up_give))
    vec_first, vec_second = by_core(grid, vectors, grid.over_core(vectors))
    tokens_both = jnp.concatenate([tokens[0], grid.over_core(tokens[0])], 0)
    cot_both = jnp.concatenate([cotangent[0], grid.over_core(cotangent[0])], 0)
    lengths_both = jnp.concatenate([lengths, grid.over_core(lengths)], 0)

    def rows_of(value, index):
        return value[index * block : (index + 1) * block]

    vec_row = jnp.concatenate([vec_first.reshape(1, -1), vec_second.reshape(1, -1)], 1)
    vec_rows = jnp.pad(vec_row, ((0, 7), (0, width - vec_row.shape[1])))
    piece_attn = jnp.concatenate(
        [
            jnp.concatenate([rows_of(trio_first, 0), rows_of(trio_first, 1)], 1),
            jnp.concatenate([rows_of(trio_second, 0), rows_of(trio_second, 1)], 1),
            jnp.concatenate([rows_of(trio_first, 2), rows_of(trio_second, 2)], 1),
            w_out,
            vec_rows,
        ],
        0,
    )
    piece_up = jnp.concatenate(
        [
            up[:, at * width : (at + 1) * width]
            for at in range(wide_blocks)
            for up in (up_first, up_second)
        ],
        0,
    )
    attn_cols = gather_chips(grid, piece_attn)
    up_cols = gather_chips(grid, piece_up)
    down_cols = gather_chips(grid, w_down)

    split_shape = (depth, SIDE, CORES, SIDE, block)
    w_qk = lay(
        grid,
        attn_cols,
        lambda col: col[:, : 2 * block].reshape(depth, CORES, block, width),
        split_shape + (width,),
    ).reshape(width, width)
    w_v = lay(
        grid,
        attn_cols,
        lambda col: jnp.stack(
            [col[:, 2 * block : 3 * block, :part], col[:, 2 * block : 3 * block, part:]], 1
        ),
        split_shape + (part,),
    ).reshape(width, part)
    w_o = lay(
        grid, attn_cols, lambda col: col[:, 3 * block : 4 * block], (depth, SIDE, SIDE, block, width)
    ).reshape(part, width)
    vec_all = lay(
        grid, attn_cols, lambda col: col[:, 4 * block : 4 * block + 1], (depth, SIDE, SIDE, 1, width)
    )
    vec_all = vec_all[..., 0, : CORES * 8 * block].reshape(depth, SIDE, SIDE, CORES, 8, block)
    vec_all = widen(vec_all.transpose(4, 0, 1, 3, 2, 5).reshape(8, width))
    ups = [
        lay(
            grid,
            up_cols,
            lambda col, at=at: col[:, 2 * at * block : 2 * (at + 1) * block].reshape(
                depth, CORES, block, width
            ),
            split_shape + (width,),
        ).reshape(width, width)
        for at in range(wide_blocks)
    ]
    downs = lay(grid, down_cols, lambda col: col, (depth, SIDE, SIDE, down_block, width)).reshape(
        hidden_part, width
    )

    inputs = widen(tokens_both)
    upstream = widen(cot_both)
    doc_ids, places = jax.vmap(partial(doc_places, count=rows))(lengths_both)
    cos_table, sin_table = rotary_tables(places, head_dim // 2)
    order = jnp.arange(rows, dtype=jnp.int32)
    visible = (doc_ids[:, :, None] == doc_ids[:, None, :]) & (
        order[None, None, :] <= order[None, :, None]
    )
    seen = visible[:, None]

    def dot(left, right):
        return jnp.dot(left, right, preferred_element_type=f32)

    def dot_back(left, right):
        return lax.dot_general(left, right, (((1,), (1,)), ((), ())), preferred_element_type=f32)

    def dot_grad(left, right):
        return lax.dot_general(
            left, right, (((0,), (0,)), ((), ())), preferred_element_type=f32
        ).astype(bf16)

    normed_one, unit_one, inv_one = norm_forward(inputs, vec_all[0], vec_all[1])
    normed_low = normed_one.astype(bf16)
    qk = dot(normed_low, w_qk)
    queries = rotate_heads(split_heads(qk[:, :part], heads), cos_table, sin_table).astype(bf16)
    keys = rotate_heads(split_heads(qk[:, part:], heads), cos_table, sin_table).astype(bf16)
    values = split_heads(dot(normed_low, w_v).astype(bf16), heads)
    scores = jnp.einsum("bqhe,bkhe->bhqk", queries, keys, preferred_element_type=f32) * scale
    scores = jnp.where(seen, scores, -1e30)
    top = jnp.max(scores, -1, keepdims=True)
    expd = jnp.exp(scores - top)
    probs = expd / jnp.sum(expd, -1, keepdims=True)
    probs_low = probs.astype(bf16)
    mixed = jnp.einsum("bhqk,bkhe->bqhe", probs_low, values, preferred_element_type=f32)
    mixed = mixed.astype(bf16).reshape(CORES * rows, part)
    branch = share(grid, dot(mixed, w_o))
    normed_two, unit_two, inv_two = norm_forward(branch, vec_all[2], vec_all[3])
    middle = inputs + normed_two
    normed_three, unit_three, inv_three = norm_forward(middle, vec_all[4], vec_all[5])
    normed_mid = normed_three.astype(bf16)
    pre = [dot(normed_mid, up) for up in ups]
    hidden = [gelu_exact(item).astype(bf16) for item in pre]
    mlp_part = sum(
        dot(item, downs[at * width : (at + 1) * width]) for at, item in enumerate(hidden)
    )
    mlp_out = share(grid, mlp_part)
    normed_four, unit_four, inv_four = norm_forward(mlp_out, vec_all[6], vec_all[7])
    result = middle[:rows] + normed_four[:rows]

    grad_mlp, grad_gain_four, grad_shift_four = norm_backward(
        upstream, unit_four, inv_four, vec_all[6]
    )
    grad_mlp_low = grad_mlp.astype(bf16)
    down_grads = jnp.concatenate([dot_grad(item, grad_mlp_low) for item in hidden], 0).reshape(
        depth, SIDE, SIDE, down_block, width
    )
    down_sum = scatter_chips(grid, lambda at_x, at_y: take(grid, down_grads, at_x, at_y))
    grad_pre = [
        (
            dot_back(grad_mlp_low, downs[at * width : (at + 1) * width]) * gelu_slope(item)
        ).astype(bf16)
        for at, item in enumerate(pre)
    ]
    up_grads = [dot_grad(normed_mid, item).reshape(split_shape + (width,)) for item in grad_pre]
    up_sum = scatter_chips(
        grid,
        lambda at_x, at_y: jnp.concatenate(
            [take(grid, item, at_x, at_y).reshape(depth, -1, width) for item in up_grads], 1
        ),
    )
    grad_norm_three = share(grid, sum(dot_back(item, up) for item, up in zip(grad_pre, ups)))
    grad_mid_part, grad_gain_three, grad_shift_three = norm_backward(
        grad_norm_three, unit_three, inv_three, vec_all[4]
    )
    grad_middle = upstream + grad_mid_part
    grad_branch, grad_gain_two, grad_shift_two = norm_backward(
        grad_middle, unit_two, inv_two, vec_all[2]
    )
    grad_branch_low = grad_branch.astype(bf16)
    out_grads = dot_grad(mixed, grad_branch_low).reshape(depth, SIDE, SIDE, block, width)
    grad_mixed = split_heads(dot_back(grad_branch_low, w_o).astype(bf16), heads)
    grad_probs = jnp.einsum("bqhe,bkhe->bhqk", grad_mixed, values, preferred_element_type=f32)
    grad_values = jnp.einsum("bhqk,bqhe->bkhe", probs_low, grad_mixed, preferred_element_type=f32)
    inner = jnp.sum(probs * grad_probs, -1, keepdims=True)
    grad_scores = (probs * (grad_probs - inner)).astype(bf16)
    grad_queries = (
        jnp.einsum("bhqk,bkhe->bqhe", grad_scores, keys, preferred_element_type=f32) * scale
    )
    grad_keys = (
        jnp.einsum("bhqk,bqhe->bkhe", grad_scores, queries, preferred_element_type=f32) * scale
    )
    grad_queries = rotate_heads(grad_queries, cos_table, -sin_table).astype(bf16)
    grad_keys = rotate_heads(grad_keys, cos_table, -sin_table).astype(bf16)
    grad_qk = jnp.concatenate(
        [grad_queries.reshape(CORES * rows, part), grad_keys.reshape(CORES * rows, part)], 1
    )
    grad_values = grad_values.astype(bf16).reshape(CORES * rows, part)
    qk_grads = dot_grad(normed_low, grad_qk).reshape(split_shape + (width,))
    v_grads = dot_grad(normed_low, grad_values).reshape(split_shape + (part,))

    def pack_attn(at_x, at_y):
        pair = take(grid, qk_grads, at_x, at_y).reshape(depth, CORES * block, width)
        single = take(grid, v_grads, at_x, at_y)
        return jnp.concatenate(
            [
                pair,
                jnp.concatenate([single[:, 0], single[:, 1]], -1),
                take(grid, out_grads, at_x, at_y),
            ],
            1,
        )

    attn_sum = scatter_chips(grid, pack_attn)
    grad_normed = share(grid, dot_back(grad_qk, w_qk) + dot_back(grad_values, w_v))
    grad_in_part, grad_gain_one, grad_shift_one = norm_backward(
        grad_normed, unit_one, inv_one, vec_all[0]
    )
    grad_input = grad_middle[:rows] + grad_in_part[:rows]

    smalls = jnp.stack(
        [
            grad_gain_one,
            grad_shift_one,
            grad_gain_two,
            grad_shift_two,
            grad_gain_three,
            grad_shift_three,
            grad_gain_four,
            grad_shift_four,
        ]
    )
    smalls = smalls + grid.over_x(smalls)
    smalls = smalls + grid.over_y(smalls)
    smalls = smalls + sum(grid.along_z(smalls, step) for step in range(1, depth))
    spot = lax.axis_index("wide") * narrow + lax.axis_index("narrow")
    smalls = lax.dynamic_slice(smalls, (0, spot * block), (8, block))

    pairs = attn_sum[: 2 * block].reshape(CORES, block, width)
    single = attn_sum[2 * block : 3 * block].reshape(block, CORES, part)
    trio_sum = jnp.concatenate([pairs, single.transpose(1, 0, 2)], 2)
    up_blocks = up_sum.reshape(wide_blocks, CORES, block, width)
    up_blocks = jnp.concatenate([up_blocks[at] for at in range(wide_blocks)], 2)

    def swap_back(value, unit):
        mine = jnp.where(is_first, value[0], value[1])
        other = grid.over_core(jnp.where(is_first, value[1], value[0]))
        even, odd = by_core(grid, mine, other)
        cut = (block, -1, unit)
        return jnp.stack([even.reshape(cut), odd.reshape(cut)], 2)

    trio_grad = swap_back(trio_sum, head_dim).reshape(block, 3, width)
    up_grad = swap_back(up_blocks, hidden_width // wide).reshape(block, hidden_width)
    return (
        result.astype(bf16)[None],
        grad_input.astype(bf16)[None],
        trio_grad[:, 0],
        trio_grad[:, 1],
        trio_grad[:, 2],
        attn_sum[3 * block : 4 * block],
        up_grad,
        down_sum,
        *[smalls[at] for at in range(8)],
    )


def solution(mesh):
    placed = (
        ROWS3,
        ROWS2,
        ROWS2,
        ROWS2,
        ROWS2,
        ROWS2,
        ROWS2,
        ROWS2,
        ROWS1,
        ROWS1,
        ROWS1,
        ROWS1,
        ROWS1,
        ROWS1,
        ROWS1,
        ROWS1,
        ROWS3,
    )
    wide, narrow = mesh.shape["wide"], mesh.shape["narrow"]
    packed = pack_fits(mesh, HEADS)
    local = partial(local_packed, wide, narrow) if packed else local_general
    return jax.shard_map(
        local,
        mesh=mesh,
        in_specs=placed,
        out_specs=(
            ROWS3,
            ROWS3,
            ROWS2,
            ROWS2,
            ROWS2,
            ROWS2,
            ROWS2,
            ROWS2,
            ROWS1,
            ROWS1,
            ROWS1,
            ROWS1,
            ROWS1,
            ROWS1,
            ROWS1,
            ROWS1,
        ),
        check_vma=False,
    )
```
